128 devices in a mesh: req: 16 (over x, z), tp: 8 (over y, core).
Axes of the slice: x: 4, y: 4, z: 4, core: 2. Of those that a mesh axis runs over, the one named last changes fastest.
Arguments:
- tokens: bfloat16 [12288, 2048], P('req'), may hold values from -6 to 6
- lengths: int32 [16, 8], P('req'), may hold values from 1 to 384, 768 in all within a row
- request_adapter: int32 [16, 8], P('req'), may hold values from 0 to 15
- w_qkv: bfloat16 [2048, 3, 2048], P('req', None, 'tp'), may hold values from -2 to 2
- w_out: bfloat16 [2048, 2048], P('tp', 'req'), may hold values from -0.125 to 0.125
- w_gate: bfloat16 [2048, 8192], P('req', 'tp'), may hold values from -0.125 to 0.125
- w_up: bfloat16 [2048, 8192], P('req', 'tp'), may hold values from -0.125 to 0.125
- w_down: bfloat16 [8192, 2048], P('tp', 'req'), may hold values from -0.0625 to 0.0625
- a_qkv: bfloat16 [2048, 256], replicated, may hold values from -0.125 to 0.125
- b_qkv: bfloat16 [256, 3, 2048], P(None, None, 'tp'), may hold values from -0.75 to 0.75
- a_out: bfloat16 [2048, 256], P('tp'), may hold values from -0.125 to 0.125
- b_out: bfloat16 [256, 2048], replicated, may hold values from -0.75 to 0.75
- a_gate: bfloat16 [2048, 256], replicated, may hold values from -0.125 to 0.125
- b_gate: bfloat16 [256, 8192], P(None, 'tp'), may hold values from -0.75 to 0.75
- a_up: bfloat16 [2048, 256], replicated, may hold values from -0.125 to 0.125
- b_up: bfloat16 [256, 8192], P(None, 'tp'), may hold values from -0.75 to 0.75
- a_down: bfloat16 [8192, 256], P('tp'), may hold values from -0.0625 to 0.0625
- b_down: bfloat16 [256, 2048], replicated, may hold values from -0.75 to 0.75
Outputs:
- layer_out: bfloat16 [12288, 2048], P('req')
The draws below stay inside these ranges and needn't reach their ends.
Inputs may be any that keep to these rules, and one draw needn't show every extreme that they name: Each row of lengths sums to 768, so the requests of one index of req fill all its slots; each row's largest length is 384.
All inputs are finite; a program needn't handle non-finite values.
Results may differ from the reference program's by a relative error of at most 0.017.
Values may be sent and summed in bfloat16 or wider, within the bound.
A program may use at most 128 MiB of HBM per device.

```python
import math
from functools import partial
import jax
import jax.numpy as jnp
import numpy as np
from jax import lax

D = 2048
H = 16
HD = 128
FF = 8192
ADAPTERS = 16
RANK = 16
TOK_DEV = 768
RPD = 8
MOST = 384
SHARDS = 16
TOKENS = 12288
N_TP = 8


def draw_w_qkv(key, part):
    noise_key = jax.random.fold_in(key, 0)
    unit_scale = 1.0 / math.sqrt(D)
    return (jax.random.truncated_normal(noise_key, -4.0, 4.0, (D, 3, D), jnp.float32) * unit_scale).astype(jnp.bfloat16)


def plant(result, key, least, high):
    index_at = [jax.random.randint(jax.random.fold_in(key, axis), (), 0, length) for axis, length in enumerate(result.shape)]
    widest = result.shape.index(max(result.shape))
    neighbour = index_at[:widest] + [(index_at[widest] + 1) % result.shape[widest]] + index_at[widest + 1:]
    return result.at[tuple(index_at)].set(least).at[tuple(neighbour)].set(high)


def levels(rng, shape, pieces, least, top_value):
    loudness, own = 1.0, jax.random.fold_in(rng, 6)
    for axis_at, blocks in pieces:
        draws = jnp.exp(jax.random.uniform(jax.random.fold_in(own, axis_at), (blocks,), jnp.float32, least / len(pieces), top_value / len(pieces)))
        loudness = loudness * jnp.repeat(draws, shape[axis_at] // blocks).reshape([-1 if axis == axis_at else 1 for axis in range(len(shape))])
    return loudness


def length_profile(count, total, reach, slope):
    portions = [(1 << 20) // math.isqrt(standing ** slope) + 1 for standing in range(2, count + 1)]
    spare, counts = total - reach - (count - 1), [1] * (count - 1)
    while spare > 0:
        movable = [i for i in range(count - 1) if counts[i] < reach]
        whole, budget = sum([portions[i] for i in movable]), spare
        for i in movable:
            addition = min(reach - counts[i], max(1, budget * portions[i] // whole), spare)
            counts[i] = counts[i] + addition
            spare = spare - addition
    return np.array([reach] + counts)


def uneven(rng, amount, total, most, slope):
    if amount == 2:
        one = jax.random.randint(rng, (), max(1, total - most), min(most, total - 1) + 1)
        return jnp.stack([one, total - one])
    sizes = jnp.asarray(length_profile(amount, total, most, slope), jnp.int32)
    twos = (amount - 1) // 2
    source_of, receiver = sizes[1:1 + 2 * twos:2], sizes[2:2 + 2 * twos:2]
    margin = jnp.minimum(source_of - 1, most - receiver)
    passed = jax.random.randint(jax.random.fold_in(rng, 1), (twos,), 0, 1 << 20) % (margin + 1)
    sizes = sizes.at[1:1 + 2 * twos:2].set(source_of - passed).at[2:2 + 2 * twos:2].set(receiver + passed)
    return sizes[jax.random.permutation(jax.random.fold_in(rng, 2), amount)]


def bell_draw(stream_key, dims, scale, most, cuts=(), held_as=jnp.bfloat16):
    values = scale * jax.random.normal(stream_key, dims, jnp.float32)
    if cuts:
        values = values * levels(stream_key, dims, cuts, -0.22, 0.18)
    return jnp.clip(values, -most, most).astype(held_as)


def setup_inputs(seed: int = 0) -> dict:
    seeds = jax.random.split(jax.random.key(seed), 19)
    return {
        "tokens": bell_draw(seeds[0], (TOKENS, D), 1.0, 6.0, ((0, 16),)),
        "lengths": jax.vmap(lambda own: uneven(own, RPD, TOK_DEV, MOST, 2))(jax.random.split(seeds[1], SHARDS)).reshape((SHARDS, RPD)).astype(jnp.int32),
        "request_adapter": plant(jax.random.randint(seeds[2], (SHARDS, RPD), 0, ADAPTERS), jax.random.fold_in(seeds[2], 1), 0, ADAPTERS - 1).astype(jnp.int32),
        "w_qkv": draw_w_qkv(jax.random.fold_in(seeds[18], 71), 0),
        "w_out": bell_draw(seeds[4], (D, D), D ** -0.5, 0.125, ((0, 8), (1, 16))),
        "w_gate": bell_draw(seeds[5], (D, FF), D ** -0.5, 0.125, ((0, 16), (1, 8))),
        "w_up": bell_draw(seeds[6], (D, FF), D ** -0.5, 0.125, ((0, 16), (1, 8))),
        "w_down": bell_draw(seeds[7], (FF, D), FF ** -0.5, 0.0625, ((0, 8), (1, 16))),
        "a_qkv": bell_draw(seeds[8], (D, ADAPTERS * RANK), D ** -0.5, 0.125),
        "b_qkv": bell_draw(seeds[9], (ADAPTERS * RANK, 3, D), (4 * RANK) ** -0.5, 0.75, ((2, 8),)),
        "a_out": bell_draw(seeds[10], (D, ADAPTERS * RANK), D ** -0.5, 0.125, ((0, 8),)),
        "b_out": bell_draw(seeds[11], (ADAPTERS * RANK, D), (4 * RANK) ** -0.5, 0.75),
        "a_gate": bell_draw(seeds[12], (D, ADAPTERS * RANK), D ** -0.5, 0.125),
        "b_gate": bell_draw(seeds[13], (ADAPTERS * RANK, FF), (4 * RANK) ** -0.5, 0.75, ((1, 8),)),
        "a_up": bell_draw(seeds[14], (D, ADAPTERS * RANK), D ** -0.5, 0.125),
        "b_up": bell_draw(seeds[15], (ADAPTERS * RANK, FF), (4 * RANK) ** -0.5, 0.75, ((1, 8),)),
        "a_down": bell_draw(seeds[16], (FF, ADAPTERS * RANK), FF ** -0.5, 0.0625, ((0, 8),)),
        "b_down": bell_draw(seeds[17], (ADAPTERS * RANK, D), (4 * RANK) ** -0.5, 0.75),
    }


epsilon = 1e-05
rope_base = 10000.0

def layer_norm(values):
    row_mean = lax.optimization_barrier(jnp.mean(values, axis=-1, keepdims=True))
    centred = values - row_mean
    spread = lax.optimization_barrier(jnp.mean(centred * centred, axis=-1, keepdims=True))
    return (centred * lax.rsqrt(spread + epsilon)).astype(jnp.bfloat16)

def slot_layout(lengths_row, adapters_row, slot_count):
    request_ends = jnp.cumsum(lengths_row).astype(jnp.int32)
    request_starts = (request_ends - lengths_row).astype(jnp.int32)
    slot_index = jnp.arange(slot_count, dtype=jnp.int32)
    request_of = lax.optimization_barrier(jnp.sum((slot_index[:, None] >= request_ends[None, :]).astype(jnp.int32), axis=1)).astype(jnp.int32)
    member = request_of[:, None] == jnp.arange(lengths_row.shape[0], dtype=jnp.int32)[None, :]
    position = (slot_index - lax.optimization_barrier(jnp.sum(jnp.where(member, request_starts[None, :], 0), axis=1))).astype(jnp.int32)
    adapter = lax.optimization_barrier(jnp.sum(jnp.where(member, adapters_row[None, :], 0), axis=1)).astype(jnp.int32)
    return (request_of, position, adapter)

def rotate(values, position):
    half_width = values.shape[-1] // 2
    frequency = jnp.exp(-math.log(rope_base) * 2.0 * jnp.arange(half_width, dtype=jnp.float32) / values.shape[-1])
    angles = position.astype(jnp.float32)[:, None] * frequency[None, :]
    cosine = jnp.cos(angles)[:, None, :]
    sine_part = jnp.sin(angles)[:, None, :]
    lower_half = values[..., :half_width]
    upper_half = values[..., half_width:]
    return jnp.concatenate([lower_half * cosine - upper_half * sine_part, upper_half * cosine + lower_half * sine_part], axis=-1)

def rounded(values):
    return lax.optimization_barrier(values.astype(jnp.bfloat16)).astype(jnp.float32)

def reference(tokens, lengths, request_adapter, w_qkv, w_out, w_gate, w_up, w_down, a_qkv, b_qkv, a_out, b_out, a_gate, b_gate, a_up, b_up, a_down, b_down):
    total_slots = tokens.shape[0]
    request_of, position, adapter = jax.vmap(partial(slot_layout, slot_count=TOK_DEV))(lengths, request_adapter)
    adapter_flat = adapter.reshape(-1)
    select = adapter_flat[:, None] == (jnp.arange(ADAPTERS * RANK, dtype=jnp.int32) // RANK)[None, :]

    def low_rank(inner, b_matrix):
        masked = jnp.where(select, inner, jnp.float32(0.0)).astype(jnp.bfloat16)
        return jnp.dot(masked, b_matrix, preferred_element_type=jnp.float32)
    normed = layer_norm(tokens.astype(jnp.float32))
    joined = jnp.dot(normed, w_qkv.reshape(D, 3 * D), preferred_element_type=jnp.float32)
    joined = joined + low_rank(jnp.dot(normed, a_qkv, preferred_element_type=jnp.float32), b_qkv.reshape(ADAPTERS * RANK, 3 * D))
    joined = joined.reshape(total_slots, 3, H, HD)
    position_flat = position.reshape(-1)
    query = rotate(joined[:, 0], position_flat).astype(jnp.bfloat16)
    key_rot = rotate(joined[:, 1], position_flat).astype(jnp.bfloat16)
    value_part = joined[:, 2].astype(jnp.bfloat16)
    score_scale = 1.0 / math.sqrt(HD)

    def attend(items):
        query_block, key_block, value_block, request_block = items
        slot_index = jnp.arange(TOK_DEV, dtype=jnp.int32)
        allowed = (request_block[:, None] == request_block[None, :]) & (slot_index[:, None] >= slot_index[None, :])
        scores = jnp.einsum('qhd,khd->hqk', query_block.astype(jnp.float32), key_block.astype(jnp.float32)) * score_scale
        scores = jnp.where(allowed[None], scores, jnp.float32(-1e+30))
        top_score = lax.optimization_barrier(jnp.max(scores, axis=-1, keepdims=True))
        expo = jnp.exp(scores - top_score)
        weights = (expo / lax.optimization_barrier(jnp.sum(expo, axis=-1, keepdims=True))).astype(jnp.bfloat16)
        mixed = jnp.einsum('hqk,khd->qhd', weights.astype(jnp.float32), value_block.astype(jnp.float32))
        return mixed.astype(jnp.bfloat16)
    attn = lax.map(attend, (query.reshape(SHARDS, TOK_DEV, H, HD), key_rot.reshape(SHARDS, TOK_DEV, H, HD), value_part.reshape(SHARDS, TOK_DEV, H, HD), request_of))
    attn_flat = attn.reshape(total_slots, D)
    group_width = D // N_TP
    attn_part = jnp.zeros((total_slots, D), jnp.float32)
    low_attn = jnp.zeros((total_slots, ADAPTERS * RANK), jnp.float32)
    for group in range(N_TP):
        columns = attn_flat[:, group * group_width:(group + 1) * group_width]
        attn_part = attn_part + rounded(jnp.dot(columns, w_out[group * group_width:(group + 1) * group_width], preferred_element_type=jnp.float32))
        low_attn = low_attn + rounded(jnp.dot(columns, a_out[group * group_width:(group + 1) * group_width], preferred_element_type=jnp.float32))
    hidden_state = tokens.astype(jnp.float32) + attn_part + low_rank(low_attn, b_out)
    normed2 = layer_norm(hidden_state)
    gate_proj = jnp.dot(normed2, w_gate, preferred_element_type=jnp.float32) + low_rank(jnp.dot(normed2, a_gate, preferred_element_type=jnp.float32), b_gate)
    up_proj = jnp.dot(normed2, w_up, preferred_element_type=jnp.float32) + low_rank(jnp.dot(normed2, a_up, preferred_element_type=jnp.float32), b_up)
    hidden = (jax.nn.silu(gate_proj) * up_proj).astype(jnp.bfloat16)
    unit_width = FF // N_TP
    down_part = jnp.zeros((total_slots, D), jnp.float32)
    low_down = jnp.zeros((total_slots, ADAPTERS * RANK), jnp.float32)
    for group in range(N_TP):
        columns = hidden[:, group * unit_width:(group + 1) * unit_width]
        down_part = down_part + rounded(jnp.dot(columns, w_down[group * unit_width:(group + 1) * unit_width], preferred_element_type=jnp.float32))
        low_down = low_down + rounded(jnp.dot(columns, a_down[group * unit_width:(group + 1) * unit_width], preferred_element_type=jnp.float32))
    return (hidden_state + down_part + low_rank(low_down, b_down)).astype(jnp.bfloat16)
```

```python
import functools
import math

import jax
import jax.numpy as jnp
from jax import lax
from jax.experimental import pallas as pl
from jax.experimental.pallas import tpu as pltpu
from jax.sharding import PartitionSpec as P

HD = 128
RANK = 16
EPS = 1e-05
BASE = 10000.0
BF = jnp.bfloat16
F32 = jnp.float32
SIDE = 4
RING_Y = 4


def mm(a, b):
    return jnp.dot(a, b, preferred_element_type=F32)


def norm_rows(x):
    mean = jnp.mean(x, axis=-1, keepdims=True)
    centred = x - mean
    spread = jnp.mean(centred * centred, axis=-1, keepdims=True)
    return (centred * lax.rsqrt(spread + EPS)).astype(BF)


def kernel(
    lens, radp, tok_h, wq_h, wo_h, wg_h, wu_h, wd_h,
    aq_h, bq_h, ao_h, bo_h, ag_h, bg_h, au_h, bu_h, ad_h, bd_h,
    out_h,
    wq, wo, wg, wu, wd, aq, bq, ao, bo, ag, bg, au, bu, ad, bd,
    tok, nrm, n2, outb, part, prx1, prx2, ps1, ps2,
    rA1, rB1, rA2, rB2, sA1, sB1, sA2, sB2, fm1, fp1, fm2, fp2,
    zq, zg, zu, zb, qkv, att, hid, hs, cosr, sinr, adp, stt,
    gs, gr, rs_s, rs_r, ag_s, ag_r, loc, osem,
):
    n_tok, dim = tok.shape
    half_tok = n_tok // 2
    blk = half_tok // RING_Y
    hd2 = dim // 2
    me_r = lax.axis_index("req")
    me_t = lax.axis_index("tp")
    xi, zi = me_r // SIDE, lax.rem(me_r, SIDE)
    yj, core = me_t // 2, lax.rem(me_t, 2)
    d = 1 - 2 * core
    xP, xM, xO = lax.rem(xi + SIDE + d, SIDE), lax.rem(xi + SIDE - d, SIDE), lax.rem(xi + 2, SIDE)
    zP, zM, zO = lax.rem(zi + SIDE + d, SIDE), lax.rem(zi + SIDE - d, SIDE), lax.rem(zi + 2, SIDE)
    yp, ym, yo = lax.rem(yj + 1, RING_Y), lax.rem(yj + 3, RING_Y), lax.rem(yj + 2, RING_Y)
    dev_xP, dev_xM = (xP * SIDE + zi, me_t), (xM * SIDE + zi, me_t)
    dev_zP, dev_zM = (xi * SIDE + zP, me_t), (xi * SIDE + zM, me_t)
    dev_yp, dev_ym = (me_r, yp * 2 + core), (me_r, ym * 2 + core)
    dev_pair = (me_r, yj * 2 + 1 - core)

    def load(i, src, dst):
        return pltpu.make_async_copy(src, dst, loc.at[i])

    loads = {}
    third = n_tok // 3
    for k in range(3):
        loads["tok%d" % k] = load(k, tok_h.at[pl.ds(k * third, third)], tok.at[pl.ds(k * third, third)])
    for k, (name, src, dst) in enumerate([
        ("aq", aq_h, aq), ("bq", bq_h, bq), ("ao", ao_h, ao), ("bo", bo_h, bo),
        ("ag", ag_h, ag), ("bg", bg_h, bg), ("au", au_h, au), ("bu", bu_h, bu),
        ("ad", ad_h, ad), ("bd", bd_h, bd),
        ("wq0", wq_h.at[0], wq.at[xi, zi, 0]), ("wq1", wq_h.at[1], wq.at[xi, zi, 1]),
        ("wo0", wo_h.at[0], wo.at[xi, zi, 0]), ("wo1", wo_h.at[1], wo.at[xi, zi, 1]),
        ("wg0", wg_h, wg.at[xi, zi]), ("wg1", wu_h, wu.at[xi, zi]),
        ("wd0", wd_h.at[0], wd.at[xi, zi, 0]), ("wd1", wd_h.at[1], wd.at[xi, zi, 1]),
    ]):
        loads[name] = load(3 + k, src, dst)
    for k in range(3):
        loads["tok%d" % k].start()
    loads["aq"].start()
    for name in ("wq0", "wq1"):
        loads[name].start()

    barrier = pltpu.get_barrier_semaphore()
    for dev in (dev_xP, dev_xM, dev_zP, dev_zM, dev_yp, dev_ym, dev_pair):
        pl.semaphore_signal(barrier, inc=1, device_id=dev, device_id_type=pl.DeviceIdType.MESH)
    pl.semaphore_wait(barrier, 7)

    def remote(src, dst, ssem, rsem, dev):
        return pltpu.make_async_remote_copy(
            src_ref=src, dst_ref=dst, send_sem=ssem, recv_sem=rsem,
            device_id=dev, device_id_type=pl.DeviceIdType.MESH)

    NAMES = ("wq", "wo", "wg", "wd")
    BUFS = {
        "wq": (lambda x, z: wq.at[x, z, 0], lambda x, z: wq.at[x, z, 1],
               lambda z: wq.at[:, z, 0], lambda x: wq.at[x, :, 1], wq_h.at[0], wq_h.at[1]),
        "wo": (lambda x, z: wo.at[x, z, 0], lambda x, z: wo.at[x, z, 1],
               lambda z: wo.at[:, z, 0], lambda x: wo.at[x, :, 1], wo_h.at[0], wo_h.at[1]),
        "wg": (lambda x, z: wg.at[x, z], lambda x, z: wu.at[x, z],
               lambda z: wg.at[:, z], lambda x: wu.at[x], wg_h, wu_h),
        "wd": (lambda x, z: wd.at[x, z, 0], lambda x, z: wd.at[x, z, 1],
               lambda z: wd.at[:, z, 0], lambda x: wd.at[x, :, 1], wd_h.at[0], wd_h.at[1]),
    }
    sent = []

    def piece(name, h, i):
        return BUFS[name][0](i, zi) if h == 0 else BUFS[name][1](xi, i)

    def group(name, h, i):
        return BUFS[name][2 + h](i)

    first = ((xi, xP, xM, xO, dev_xP, dev_xM), (zi, zP, zM, zO, dev_zP, dev_zM))
    second = (first[1], first[0])

    def wcopy(name, h, kind, where, src=None):
        w = NAMES.index(name)
        o, p_, m_, opp, dev_p, dev_m = (first if kind < 3 else second)[h]
        ref = (piece if kind < 3 else group)(name, h, where)
        dev = dev_m if kind in (1, 4) else dev_p
        return remote(ref if src is None else src, ref, gs.at[w, h, kind], gr.at[w, h, kind], dev)

    def start(c):
        c.start()
        sent.append(c)

    def g_own(name):
        for h in range(2):
            o = first[h][0]
            for kind in (0, 1):
                start(wcopy(name, h, kind, o, src=BUFS[name][4 + h]))

    def g_f1(name):
        for h in range(2):
            m_ = first[h][2]
            wcopy(name, h, 0, m_).wait_recv()
            start(wcopy(name, h, 2, m_))

    def g_s2(name):
        for h in range(2):
            loads[name + str(h)].wait()
            wcopy(name, h, 1, first[h][1]).wait_recv()
            wcopy(name, h, 2, first[h][3]).wait_recv()
            start(wcopy(name, h, 3, second[h][0]))
            start(wcopy(name, h, 4, second[h][0]))

    def g_f2(name):
        for h in range(2):
            m_ = second[h][2]
            wcopy(name, h, 3, m_).wait_recv()
            start(wcopy(name, h, 5, m_))

    def g_done(name):
        for h in range(2):
            wcopy(name, h, 4, second[h][1]).wait_recv()
            wcopy(name, h, 5, second[h][3]).wait_recv()

    g_own("wq")
    g_own("wo")
    g_own("wg")
    for name in ("bq", "ao", "bo", "ag", "bg", "au", "bu", "ad", "bd", "wo0", "wo1", "wg0", "wg1", "wd0", "wd1"):
        loads[name].start()

    lane = lax.broadcasted_iota(jnp.int32, (blk, HD), 1)
    lane_half = lax.rem(lane, HD // 2)
    freq = jnp.exp(-math.log(BASE) * 2.0 * lane_half.astype(F32) / HD)
    sign = jnp.where(lane < HD // 2, -1.0, 1.0)
    n_req = lens.shape[1]

    @pl.loop(0, n_tok // blk)
    def _(i):
        rows = pl.ds(pl.multiple_of(i * blk, blk), blk)
        slot = lax.broadcasted_iota(jnp.int32, (blk, HD), 0) + i * blk
        begin = jnp.zeros((blk, HD), jnp.int32)
        which = jnp.full((blk, HD), radp[0, 0], jnp.int32)
        end = lens[0, 0]
        for r in range(n_req - 1):
            past = slot >= end
            begin = jnp.where(past, end, begin)
            which = jnp.where(past, radp[0, r + 1], which)
            end = end + lens[0, r + 1]
        angle = (slot - begin).astype(F32) * freq
        cosr[rows, :] = jnp.cos(angle)
        sinr[rows, :] = jnp.sin(angle) * sign
        adp[rows, :] = which
        stt[rows, :] = begin

    def keep(z, rows):
        which = adp[rows, :]
        reps = z.shape[1] // HD
        which = jnp.concatenate([which] * reps, axis=1)
        col = lax.broadcasted_iota(jnp.int32, z.shape, 1) // RANK
        return jnp.where(which == col, z, 0.0).astype(BF)

    g_f1("wq")

    ln_rows = 32
    for k in range(3):
        loads["tok%d" % k].wait()

        @pl.loop(0, third // ln_rows)
        def _(i):
            rows = pl.ds(pl.multiple_of(k * third + i * ln_rows, ln_rows), ln_rows)
            nrm[rows, :] = norm_rows(tok[rows, :].astype(F32))

        if k == 0:
            g_s2("wq")
            g_f1("wo")
            g_f1("wg")
    loads["aq"].wait()

    @pl.loop(0, 2)
    def _(i):
        rows = pl.ds(pl.multiple_of(i * half_tok, half_tok), half_tok)
        zq[rows, :] = keep(mm(nrm[rows, :], aq[...]), rows)

    g_f2("wq")
    g_s2("wo")
    loads["bq"].wait()
    g_own("wd")
    g_s2("wg")
    g_done("wq")

    width = wq.shape[-1] // 3

    for i in range(3):
        wcol = wq[:, :, :, :, i * width:(i + 1) * width].reshape(dim, width)
        bcol = bq[:, i * width:(i + 1) * width]
        for t in range(2):
            rows = pl.ds(t * half_tok, half_tok)
            acc = mm(nrm[rows, :], wcol) + mm(zq[rows, :], bcol)
            for h in range(width // HD):
                part_h = acc[:, h * HD:(h + 1) * HD]
                if i < 2:
                    part_h = part_h * cosr[rows, :] + pltpu.roll(part_h, HD // 2, axis=1) * sinr[rows, :]
                qkv[i, h, rows, :] = part_h.astype(BF)
    g_f2("wo")
    g_f1("wd")

    tile = n_tok // 3
    scale = 1.0 / math.sqrt(HD)
    for h in range(width // HD):
        for b in range(3):
            q0 = b * tile
            k0 = max(0, q0 - half_tok)
            klen = q0 + tile - k0
            q = qkv[0, h, q0:q0 + tile, :]
            kk = qkv[1, h, k0:k0 + klen, :]
            s = lax.dot_general(q, kk, (((1,), (1,)), ((), ())), preferred_element_type=F32) * scale
            qpos = lax.broadcasted_iota(jnp.int32, s.shape, 0) + q0
            kpos = lax.broadcasted_iota(jnp.int32, s.shape, 1) + k0
            begin = jnp.concatenate([stt[q0:q0 + tile, :]] * (klen // HD), axis=1)
            s = jnp.where((kpos <= qpos) & (kpos >= begin), s, -1e30)
            e = jnp.exp(s - jnp.max(s, axis=-1, keepdims=True))
            w = (e / jnp.sum(e, axis=-1, keepdims=True)).astype(BF)
            att[q0:q0 + tile, h * HD:(h + 1) * HD] = mm(w, qkv[2, h, k0:k0 + klen, :]).astype(BF)

    def project(rows, act, a_mat, b_mat, wbuf):
        zb[rows, :] = keep(mm(act[rows, :], a_mat[...]), rows)

        @pl.loop(0, SIDE)
        def _(x):
            kdim = act.shape[1]
            cols = [wbuf[x, z].reshape(kdim, HD) for z in range(SIDE)]
            n = pl.ds(pl.multiple_of(x * SIDE * HD, SIDE * HD), SIDE * HD)
            acc = mm(act[rows, :], jnp.concatenate(cols, axis=1)) + mm(zb[rows, :], b_mat[:, n])
            part[rows, n] = acc.astype(BF)

    class Reduce:
        def __init__(self, which, prx, ps, rA, rB, sA, sB, fm, fp):
            self.w, self.prx, self.ps = which, prx, ps
            self.rA, self.rB, self.sA, self.sB, self.fm, self.fp = rA, rB, sA, sB, fm, fp
            self.order = (yo, yp, ym, yj)

        def c(self, i, src, dst, dev):
            return remote(src, dst, rs_s.at[self.w, i], rs_r.at[self.w, i], dev)

        def rows(self, c, j):
            return pl.ds(pl.multiple_of(c * half_tok + j * blk, blk), blk)

        def pair(self, k):
            j = self.order[k]
            return self.c(k, part.at[self.rows(1 - core, j)], self.prx.at[j], dev_pair)

        def send_pair(self):
            for k in range(4):
                start(self.pair(k))

        def combine(self, k):
            j = self.order[k]
            self.pair(k).wait_recv()
            s = part[self.rows(core, j), :].astype(F32) + self.prx[j].astype(F32)
            self.ps[j] = s.astype(BF)

        def ring1(self):
            A, B = pl.ds(0, hd2), pl.ds(hd2, hd2)
            self.combine(0)
            start(self.c(4, self.ps.at[yo, :, A], self.rA, dev_yp))
            start(self.c(5, self.ps.at[yo, :, B], self.rB, dev_ym))
            self.combine(1)
            start(self.c(6, self.ps.at[yp, :, B], self.fm.at[:, B], dev_yp))
            self.combine(2)
            start(self.c(7, self.ps.at[ym, :, A], self.fp.at[:, A], dev_ym))

        def ring2(self):
            A, B = pl.ds(0, hd2), pl.ds(hd2, hd2)
            self.c(4, self.sA, self.rA, dev_yp).wait_recv()
            self.sA[...] = (self.ps[yp, :, A].astype(F32) + self.rA[...].astype(F32)).astype(BF)
            start(self.c(8, self.sA, self.fm.at[:, A], dev_yp))
            self.c(5, self.sB, self.rB, dev_ym).wait_recv()
            self.sB[...] = (self.ps[ym, :, B].astype(F32) + self.rB[...].astype(F32)).astype(BF)
            start(self.c(9, self.sB, self.fp.at[:, B], dev_ym))
            self.pair(3).wait_recv()

        def finish(self):
            A, B = pl.ds(0, hd2), pl.ds(hd2, hd2)
            self.c(6, self.fm.at[:, B], self.fm.at[:, B], dev_yp).wait_recv()
            self.c(7, self.fp.at[:, A], self.fp.at[:, A], dev_ym).wait_recv()
            self.c(8, self.sA, self.fm.at[:, A], dev_yp).wait_recv()
            self.c(9, self.sB, self.fp.at[:, B], dev_ym).wait_recv()

        def own(self, r0, n):
            own_rows = pl.ds(pl.multiple_of(core * half_tok + yj * blk + r0, n), n)
            r = pl.ds(pl.multiple_of(r0, n), n)
            return (part[own_rows, :].astype(F32) + self.prx[yj, r].astype(F32)
                    + self.fm[r, :].astype(F32) + self.fp[r, :].astype(F32))

    class Spread:
        def __init__(self, which, buf):
            self.w, self.buf = which, buf

        def c(self, i, rows, dev, cols=None):
            ref = self.buf.at[rows] if cols is None else self.buf.at[rows, cols]
            return remote(ref, ref, ag_s.at[self.w, i], ag_r.at[self.w, i], dev)

        def rows(self, c, j):
            return pl.ds(pl.multiple_of(c * half_tok + j * blk, blk), blk)

        def first(self):
            mine = self.rows(core, yj)
            start(self.c(0, mine, dev_yp))
            start(self.c(1, mine, dev_ym))
            start(self.c(2, mine, dev_pair))

        def relay(self):
            A, B = pl.ds(0, hd2), pl.ds(hd2, hd2)
            self.c(0, self.rows(core, ym), dev_yp).wait_recv()
            start(self.c(3, self.rows(core, ym), dev_yp, A))
            start(self.c(4, self.rows(core, ym), dev_pair))
            self.c(1, self.rows(core, yp), dev_ym).wait_recv()
            start(self.c(5, self.rows(core, yp), dev_ym, B))
            start(self.c(6, self.rows(core, yp), dev_pair))

        def relay2(self):
            A, B = pl.ds(0, hd2), pl.ds(hd2, hd2)
            self.c(3, self.rows(core, yo), dev_yp, A).wait_recv()
            start(self.c(7, self.rows(core, yo), dev_pair, A))
            self.c(5, self.rows(core, yo), dev_ym, B).wait_recv()
            start(self.c(8, self.rows(core, yo), dev_pair, B))

        def finish(self):
            A, B = pl.ds(0, hd2), pl.ds(hd2, hd2)
            self.c(2, self.rows(1 - core, yj), dev_pair).wait_recv()
            self.c(4, self.rows(1 - core, ym), dev_pair).wait_recv()
            self.c(6, self.rows(1 - core, yp), dev_pair).wait_recv()
            self.c(7, self.rows(1 - core, yo), dev_pair, A).wait_recv()
            self.c(8, self.rows(1 - core, yo), dev_pair, B).wait_recv()

    other = pl.ds(pl.multiple_of((1 - core) * half_tok, half_tok), half_tok)
    ours = pl.ds(pl.multiple_of(core * half_tok, half_tok), half_tok)
    mine_rows = core * half_tok + yj * blk

    for name in ("ao", "bo"):
        loads[name].wait()
    g_done("wo")
    red1 = Reduce(0, prx1, ps1, rA1, rB1, sA1, sB1, fm1, fp1)
    project(other, att, ao, bo, wo)
    red1.send_pair()
    project(ours, att, ao, bo, wo)
    red1.ring1()
    g_f2("wg")
    g_s2("wd")
    red1.ring2()
    red1.finish()

    own_rows = 16
    spread1 = Spread(0, n2)

    @pl.loop(0, blk // own_rows)
    def _(i):
        r0 = i * own_rows
        src = pl.ds(pl.multiple_of(mine_rows + r0, own_rows), own_rows)
        h_new = tok[src, :].astype(F32) + red1.own(r0, own_rows)
        hs[pl.ds(pl.multiple_of(r0, own_rows), own_rows), :] = h_new
        n2[src, :] = norm_rows(h_new)

    spread1.first()
    spread1.relay()
    spread1.relay2()
    g_f2("wd")
    for name in ("ag", "bg", "au", "bu", "ad", "bd"):
        loads[name].wait()
    spread1.finish()

    @pl.loop(0, 2)
    def _(i):
        rows = pl.ds(pl.multiple_of(i * half_tok, half_tok), half_tok)
        zg[rows, :] = keep(mm(n2[rows, :], ag[...]), rows)
        zu[rows, :] = keep(mm(n2[rows, :], au[...]), rows)

    g_done("wg")
    ff = wg.shape[-1]
    ft = 256

    @pl.loop(0, ff // ft)
    def _(f):
        cols = pl.ds(pl.multiple_of(f * ft, ft), ft)
        wgc = wg[:, :, :, cols].reshape(dim, ft)
        wuc = wu[:, :, :, cols].reshape(dim, ft)
        for t in range(2):
            rows = pl.ds(t * half_tok, half_tok)
            g = mm(n2[rows, :], wgc) + mm(zg[rows, :], bg[:, cols])
            u = mm(n2[rows, :], wuc) + mm(zu[rows, :], bu[:, cols])
            hid[rows, cols] = (g / (1.0 + jnp.exp(-g)) * u).astype(BF)

    g_done("wd")
    for c in sent:
        c.wait_send()
    sent.clear()
    red2 = Reduce(1, prx2, ps2, rA2, rB2, sA2, sB2, fm2, fp2)
    project(other, hid, ad, bd, wd)
    red2.send_pair()
    project(ours, hid, ad, bd, wd)
    red2.ring1()
    red2.ring2()
    red2.finish()
    spread2 = Spread(1, outb)

    @pl.loop(0, blk // own_rows)
    def _(i):
        r0 = i * own_rows
        src = pl.ds(pl.multiple_of(mine_rows + r0, own_rows), own_rows)
        h_old = hs[pl.ds(pl.multiple_of(r0, own_rows), own_rows), :]
        outb[src, :] = (h_old + red2.own(r0, own_rows)).astype(BF)

    spread2.first()
    spread2.relay()
    spread2.relay2()
    o1 = pltpu.make_async_copy(outb.at[ours], out_h.at[ours], osem.at[0])
    o1.start()
    spread2.finish()
    o2 = pltpu.make_async_copy(outb.at[other], out_h.at[other], osem.at[1])
    o2.start()
    o1.wait()
    o2.wait()
    for c in sent:
        c.wait_send()


def body(
    tokens, lengths, request_adapter, w_qkv, w_out, w_gate, w_up, w_down,
    a_qkv, b_qkv, a_out, b_out, a_gate, b_gate, a_up, b_up, a_down, b_down,
):
    n_tok, dim = tokens.shape
    kq, _, lw = w_qkv.shape
    ff = w_gate.shape[1]
    nz = a_qkv.shape[1]
    blk = n_tok // 8
    V = pltpu.VMEM
    scratch = [
        V((SIDE, SIDE, 2, kq // 2, 3 * lw), BF),
        V((SIDE, SIDE, 2, w_out.shape[0] // 2, w_out.shape[1]), BF),
        V((SIDE, SIDE, w_gate.shape[0], ff), BF),
        V((SIDE, SIDE, w_up.shape[0], ff), BF),
        V((SIDE, SIDE, 2, w_down.shape[0] // 2, w_down.shape[1]), BF),
        V(a_qkv.shape, BF), V((nz, 3 * lw), BF), V(a_out.shape, BF), V(b_out.shape, BF),
        V(a_gate.shape, BF), V(b_gate.shape, BF), V(a_up.shape, BF), V(b_up.shape, BF),
        V(a_down.shape, BF), V(b_down.shape, BF),
        V((n_tok, dim), BF), V((n_tok, dim), BF), V((n_tok, dim), BF), V((n_tok, dim), BF), V((n_tok, dim), BF),
        V((4, blk, dim), BF), V((4, blk, dim), BF), V((4, blk, dim), BF), V((4, blk, dim), BF),
    ]
    scratch += [V((blk, dim // 2), BF)] * 8
    scratch += [V((blk, dim), BF)] * 4
    scratch += [
        V((n_tok, nz), BF), V((n_tok, nz), BF), V((n_tok, nz), BF), V((n_tok, nz), BF),
        V((3, lw // HD, n_tok, HD), BF), V((n_tok, lw), BF), V((n_tok, ff), BF), V((blk, dim), F32),
        V((n_tok, HD), F32), V((n_tok, HD), F32), V((n_tok, HD), jnp.int32), V((n_tok, HD), jnp.int32),
    ]
    D = pltpu.SemaphoreType.DMA
    scratch += [D((4, 2, 6)), D((4, 2, 6)), D((2, 10)), D((2, 10)), D((2, 9)), D((2, 9)), D((24,)), D((2,))]
    smem = pl.BlockSpec(memory_space=pltpu.SMEM)
    hbm = pl.BlockSpec(memory_space=pl.ANY)
    return pl.pallas_call(
        kernel,
        out_shape=jax.ShapeDtypeStruct((n_tok, dim), BF),
        in_specs=[smem, smem] + [hbm] * 16,
        out_specs=hbm,
        scratch_shapes=scratch,
        compiler_params=pltpu.CompilerParams(
            collective_id=0, has_side_effects=True, vmem_limit_bytes=67043328),
        name="layer",
    )(
        lengths, request_adapter, tokens,
        w_qkv.reshape(2, kq // 2, 3 * lw),
        w_out.reshape(2, w_out.shape[0] // 2, w_out.shape[1]),
        w_gate, w_up,
        w_down.reshape(2, w_down.shape[0] // 2, w_down.shape[1]),
        a_qkv, b_qkv.reshape(nz, 3 * lw), a_out, b_out, a_gate, b_gate, a_up, b_up, a_down, b_down,
    )


def solution(mesh):
    in_specs = (
        P("req", None), P("req", None), P("req", None), P("req", None, "tp"), P("tp", "req"),
        P("req", "tp"), P("req", "tp"), P("tp", "req"), P(), P(None, None, "tp"), P("tp", None),
        P(), P(), P(None, "tp"), P(), P(None, "tp"), P("tp", None), P(),
    )
    return jax.shard_map(body, mesh=mesh, in_specs=in_specs, out_specs=P("req", None), check_vma=False)
```

```python
import functools
import math

import jax
import jax.numpy as jnp
from jax import lax
from jax.experimental import pallas as pl
from jax.experimental.pallas import tpu as pltpu
from jax.sharding import PartitionSpec as P

HD = 128
RANK = 16
EPS = 1e-05
BASE = 10000.0
BF = jnp.bfloat16
F32 = jnp.float32
SIDE = 4
RING_Y = 4


def mm(a, b):
    return jnp.dot(a, b, preferred_element_type=F32)


def norm_rows(x):
    mean = jnp.mean(x, axis=-1, keepdims=True)
    centred = x - mean
    spread = jnp.mean(centred * centred, axis=-1, keepdims=True)
    return (centred * lax.rsqrt(spread + EPS)).astype(BF)


def kernel(
    lens, radp, tok_h, wq_h, wo_h, wg_h, wu_h, wd_h,
    aq_h, bq_h, ao_h, bo_h, ag_h, bg_h, au_h, bu_h, ad_h, bd_h,
    out_h,
    wq, wo, wg, wu, wd, aq, bq, ao, bo, ag, bg, au, bu, ad, bd,
    tok, nrm, n2, outb, part1, part2, prx1, prx2, ps1, ps2,
    rA1, rB1, rA2, rB2, sA1, sB1, sA2, sB2, fm1, fp1, fm2, fp2,
    zq, zg, zu, zb, zd, qkv, att, hid, hs, cosr, sinr, adp, stt,
    gs, gr, rs1_s, rs1_r, ag1_s, ag1_r, rs2_s, rs2_r, ag2_s, ag2_r, loc, osem,
):
    n_tok, dim = tok.shape
    half_tok = n_tok // 2
    blk = half_tok // RING_Y
    hd2 = dim // 2
    me_r = lax.axis_index("req")
    me_t = lax.axis_index("tp")
    xi, zi = me_r // SIDE, lax.rem(me_r, SIDE)
    yj, core = me_t // 2, lax.rem(me_t, 2)
    d = 1 - 2 * core
    xP, xM, xO = lax.rem(xi + SIDE + d, SIDE), lax.rem(xi + SIDE - d, SIDE), lax.rem(xi + 2, SIDE)
    zP, zM, zO = lax.rem(zi + SIDE + d, SIDE), lax.rem(zi + SIDE - d, SIDE), lax.rem(zi + 2, SIDE)
    yp, ym, yo = lax.rem(yj + 1, RING_Y), lax.rem(yj + 3, RING_Y), lax.rem(yj + 2, RING_Y)
    dev_xP, dev_xM = (xP * SIDE + zi, me_t), (xM * SIDE + zi, me_t)
    dev_zP, dev_zM = (xi * SIDE + zP, me_t), (xi * SIDE + zM, me_t)
    dev_yp, dev_ym = (me_r, yp * 2 + core), (me_r, ym * 2 + core)
    dev_pair = (me_r, yj * 2 + 1 - core)
    par = lax.rem(xi + zi, 2)

    def pick(a, b):
        return a + par * (b - a)

    src_i, src_g, rel_g = pick(xi, zi), pick(zi, xi), pick(xi, zi)
    srcO = pick(xO, zO)
    relP, relM = pick(zP, xP), pick(zM, xM)
    src_dP = (pick(xP * SIDE + zi, xi * SIDE + zP), me_t)
    src_dM = (pick(xM * SIDE + zi, xi * SIDE + zM), me_t)
    rel_dP = (pick(xi * SIDE + zP, xP * SIDE + zi), me_t)
    rel_dM = (pick(xi * SIDE + zM, xM * SIDE + zi), me_t)

    def load(i, src, dst):
        return pltpu.make_async_copy(src, dst, loc.at[i])

    loads = {}
    khalf = wq.shape[3] // 2
    third = n_tok // 3
    for k in range(3):
        loads["tok%d" % k] = load(k, tok_h.at[pl.ds(k * third, third)], tok.at[pl.ds(k * third, third)])
    for k, (name, src, dst) in enumerate([
        ("aq", aq_h, aq), ("bq", bq_h, bq), ("ao", ao_h, ao), ("bo", bo_h, bo),
        ("ag", ag_h, ag), ("bg", bg_h, bg), ("au", au_h, au), ("bu", bu_h, bu),
        ("ad", ad_h, ad), ("bd", bd_h, bd),
        ("wq0", wq_h.at[:, :khalf], wq.at[xi, zi, :, :khalf]),
        ("wq1", wq_h.at[:, khalf:], wq.at[xi, zi, :, khalf:]),
        ("wo0", wo_h.at[0], wo.at[xi, zi, 0]), ("wo1", wo_h.at[1], wo.at[xi, zi, 1]),
        ("wg0", wg_h, wg.at[xi, zi]), ("wg1", wu_h, wu.at[xi, zi]),
        ("wd", wd_h, wd.at[par, src_g, src_i // 2]),
    ]):
        loads[name] = load(3 + k, src, dst)
    for k in range(3):
        loads["tok%d" % k].start()
    loads["aq"].start()
    for name in ("wq0", "wq1"):
        loads[name].start()

    barrier = pltpu.get_barrier_semaphore()
    for dev in (dev_xP, dev_xM, dev_zP, dev_zM, dev_yp, dev_ym, dev_pair):
        pl.semaphore_signal(barrier, inc=1, device_id=dev, device_id_type=pl.DeviceIdType.MESH)
    pl.semaphore_wait(barrier, 7)

    def remote(src, dst, ssem, rsem, dev):
        return pltpu.make_async_remote_copy(
            src_ref=src, dst_ref=dst, send_sem=ssem, recv_sem=rsem,
            device_id=dev, device_id_type=pl.DeviceIdType.MESH)

    NAMES = ("wq", "wo", "wg", "wd")
    BUFS = {
        "wq": (lambda x, z: wq.at[x, z, :, :khalf], lambda x, z: wq.at[x, z, :, khalf:],
               lambda z: wq.at[:, z, :, :khalf], lambda x: wq.at[x, :, :, khalf:],
               wq_h.at[:, :khalf], wq_h.at[:, khalf:]),
        "wo": (lambda x, z: wo.at[x, z, 0], lambda x, z: wo.at[x, z, 1],
               lambda z: wo.at[:, z, 0], lambda x: wo.at[x, :, 1], wo_h.at[0], wo_h.at[1]),
        "wg": (lambda x, z: wg.at[x, z], lambda x, z: wu.at[x, z],
               lambda z: wg.at[:, z], lambda x: wu.at[x], wg_h, wu_h),
        "wd": (None, None, lambda z: wd.at[0, z], lambda x: wd.at[1, x], None, None),
    }
    sent = []

    def piece(name, h, i):
        return BUFS[name][0](i, zi) if h == 0 else BUFS[name][1](xi, i)

    def group(name, h, i):
        return BUFS[name][2 + h](i)

    first = ((xi, xP, xM, xO, dev_xP, dev_xM), (zi, zP, zM, zO, dev_zP, dev_zM))
    second = (first[1], first[0])

    def wcopy(name, h, kind, where, src=None):
        w = NAMES.index(name)
        o, p_, m_, opp, dev_p, dev_m = (first if kind < 3 else second)[h]
        ref = (piece if kind < 3 else group)(name, h, where)
        dev = dev_m if kind in (1, 4) else dev_p
        return remote(ref if src is None else src, ref, gs.at[w, h, kind], gr.at[w, h, kind], dev)

    def start(c):
        c.start()
        sent.append(c)

    def g_own(name):
        for h in range(2):
            o = first[h][0]
            for kind in (0, 1):
                start(wcopy(name, h, kind, o, src=BUFS[name][4 + h]))

    def g_f1(name):
        for h in range(2):
            m_ = first[h][2]
            wcopy(name, h, 0, m_).wait_recv()
            start(wcopy(name, h, 2, m_))

    def g_s2(name):
        for h in range(2):
            loads[name + str(h)].wait()
            wcopy(name, h, 1, first[h][1]).wait_recv()
            wcopy(name, h, 2, first[h][3]).wait_recv()
            start(wcopy(name, h, 3, second[h][0]))
            start(wcopy(name, h, 4, second[h][0]))

    def g_f2(name):
        for h in range(2):
            m_ = second[h][2]
            wcopy(name, h, 3, m_).wait_recv()
            start(wcopy(name, h, 5, m_))

    def g_done(name):
        for h in range(2):
            wcopy(name, h, 4, second[h][1]).wait_recv()
            wcopy(name, h, 5, second[h][3]).wait_recv()

    def d_copy(kind, stream, g, i, dev, src=None):
        ref = wd.at[stream, g, i // 2]
        return remote(ref if src is None else src, ref, gs.at[3, 0, kind], gr.at[3, 0, kind], dev)

    def d_own():
        start(d_copy(0, par, src_g, src_i, src_dP, wd_h))
        start(d_copy(1, par, src_g, src_i, src_dM, wd_h))

    def d_f1():
        d_copy(0, 1 - par, rel_g, relM, rel_dP).wait_recv()
        start(d_copy(2, 1 - par, rel_g, relM, rel_dP))

    def d_s2():
        loads["wd"].wait()
        d_copy(1, 1 - par, rel_g, relP, rel_dM).wait_recv()
        d_copy(2, par, src_g, srcO, src_dP).wait_recv()
        for h in range(2):
            start(wcopy("wd", h, 3, second[h][0]))
            start(wcopy("wd", h, 4, second[h][0]))

    def d_got(kind):
        for h in range(2):
            wcopy("wd", h, kind, second[h][1 if kind == 4 else 3]).wait_recv()

    g_own("wq")
    g_own("wo")
    g_own("wg")
    for name in ("bq", "ao", "bo", "ag", "bg", "au", "bu", "ad", "bd", "wo0", "wo1", "wg0", "wg1", "wd"):
        loads[name].start()

    lane = lax.broadcasted_iota(jnp.int32, (blk, HD), 1)
    lane_half = lax.rem(lane, HD // 2)
    freq = jnp.exp(-math.log(BASE) * 2.0 * lane_half.astype(F32) / HD)
    sign = jnp.where(lane < HD // 2, -1.0, 1.0)
    n_req = lens.shape[1]

    @pl.loop(0, n_tok // blk)
    def _(i):
        rows = pl.ds(pl.multiple_of(i * blk, blk), blk)
        slot = lax.broadcasted_iota(jnp.int32, (blk, HD), 0) + i * blk
        begin = jnp.zeros((blk, HD), jnp.int32)
        which = jnp.full((blk, HD), radp[0, 0], jnp.int32)
        end = lens[0, 0]
        for r in range(n_req - 1):
            past = slot >= end
            begin = jnp.where(past, end, begin)
            which = jnp.where(past, radp[0, r + 1], which)
            end = end + lens[0, r + 1]
        angle = (slot - begin).astype(F32) * freq
        cosr[rows, :] = jnp.cos(angle)
        sinr[rows, :] = jnp.sin(angle) * sign
        adp[rows, :] = which
        stt[rows, :] = begin

    def keep(z, rows):
        which = adp[rows, :]
        reps = z.shape[1] // HD
        which = jnp.concatenate([which] * reps, axis=1)
        col = lax.broadcasted_iota(jnp.int32, z.shape, 1) // RANK
        return jnp.where(which == col, z, 0.0).astype(BF)

    g_f1("wq")

    ln_rows = 32
    for k in range(3):
        loads["tok%d" % k].wait()

        @pl.loop(0, third // ln_rows)
        def _(i):
            rows = pl.ds(pl.multiple_of(k * third + i * ln_rows, ln_rows), ln_rows)
            nrm[rows, :] = norm_rows(tok[rows, :].astype(F32))

        if k == 0:
            g_s2("wq")
            g_f1("wo")
            g_f1("wg")
    loads["aq"].wait()

    @pl.loop(0, 2)
    def _(i):
        rows = pl.ds(pl.multiple_of(i * half_tok, half_tok), half_tok)
        zq[rows, :] = keep(mm(nrm[rows, :], aq[...]), rows)

    g_f2("wq")
    g_s2("wo")
    loads["bq"].wait()
    d_own()
    g_s2("wg")
    g_done("wq")

    width = wq.shape[-1]

    for i in range(3):
        wcol = wq[:, :, i].reshape(dim, width)
        bcol = bq[i]
        for t in range(2):
            rows = pl.ds(t * half_tok, half_tok)
            acc = mm(nrm[rows, :], wcol) + mm(zq[rows, :], bcol)
            for h in range(width // HD):
                part_h = acc[:, h * HD:(h + 1) * HD]
                if i < 2:
                    part_h = part_h * cosr[rows, :] + pltpu.roll(part_h, HD // 2, axis=1) * sinr[rows, :]
                qkv[i, h, rows, :] = part_h.astype(BF)
    g_f2("wo")
    d_f1()

    tile = n_tok // 3
    scale = 1.0 / math.sqrt(HD)
    for h in range(width // HD):
        for b in range(3):
            q0 = b * tile
            k0 = max(0, q0 - half_tok)
            klen = q0 + tile - k0
            q = qkv[0, h, q0:q0 + tile, :]
            kk = qkv[1, h, k0:k0 + klen, :]
            s = lax.dot_general(q, kk, (((1,), (1,)), ((), ())), preferred_element_type=F32) * scale
            qpos = lax.broadcasted_iota(jnp.int32, s.shape, 0) + q0
            kpos = lax.broadcasted_iota(jnp.int32, s.shape, 1) + k0
            begin = jnp.concatenate([stt[q0:q0 + tile, :]] * (klen // HD), axis=1)
            s = jnp.where((kpos <= qpos) & (kpos >= begin), s, -1e30)
            e = jnp.exp(s - jnp.max(s, axis=-1, keepdims=True))
            w = (e / jnp.sum(e, axis=-1, keepdims=True)).astype(BF)
            att[q0:q0 + tile, h * HD:(h + 1) * HD] = mm(w, qkv[2, h, k0:k0 + klen, :]).astype(BF)

    class Reduce:
        def __init__(self, part, prx, ps, rA, rB, sA, sB, fm, fp, ssem, rsem):
            self.part, self.prx, self.ps = part, prx, ps
            self.rA, self.rB, self.sA, self.sB, self.fm, self.fp = rA, rB, sA, sB, fm, fp
            self.ssem, self.rsem = ssem, rsem
            self.order = (yo, yp, ym, yj)
            hw = fm.shape[-1] // 2
            self.A, self.B = pl.ds(0, hw), pl.ds(hw, hw)

        def c(self, i, src, dst, dev):
            return remote(src, dst, self.ssem.at[i], self.rsem.at[i], dev)

        def pair(self, k):
            j = self.order[k]
            return self.c(k, self.part(1 - core, j), self.prx.at[j], dev_pair)

        def send_pair(self):
            for k in range(4):
                start(self.pair(k))

        def combine(self, k):
            j = self.order[k]
            self.pair(k).wait_recv()
            self.ps[j] = (self.part(core, j)[...].astype(F32) + self.prx[j].astype(F32)).astype(BF)

        def ring1(self):
            A, B = self.A, self.B
            self.combine(0)
            start(self.c(4, self.ps.at[yo, ..., A], self.rA, dev_yp))
            start(self.c(5, self.ps.at[yo, ..., B], self.rB, dev_ym))
            self.combine(1)
            start(self.c(6, self.ps.at[yp, ..., B], self.fm.at[..., B], dev_yp))
            self.combine(2)
            start(self.c(7, self.ps.at[ym, ..., A], self.fp.at[..., A], dev_ym))

        def ring2(self):
            A, B = self.A, self.B
            self.c(4, self.sA, self.rA, dev_yp).wait_recv()
            self.sA[...] = (self.ps[yp, ..., A].astype(F32) + self.rA[...].astype(F32)).astype(BF)
            start(self.c(8, self.sA, self.fm.at[..., A], dev_yp))
            self.c(5, self.sB, self.rB, dev_ym).wait_recv()
            self.sB[...] = (self.ps[ym, ..., B].astype(F32) + self.rB[...].astype(F32)).astype(BF)
            start(self.c(9, self.sB, self.fp.at[..., B], dev_ym))

        def finish(self):
            A, B = self.A, self.B
            self.pair(3).wait_recv()
            self.c(6, self.fm.at[..., B], self.fm.at[..., B], dev_yp).wait_recv()
            self.c(7, self.fp.at[..., A], self.fp.at[..., A], dev_ym).wait_recv()
            self.c(8, self.sA, self.fm.at[..., A], dev_yp).wait_recv()
            self.c(9, self.sB, self.fp.at[..., B], dev_ym).wait_recv()

        def total(self, r):
            return (self.part(core, yj)[r].astype(F32) + self.prx[yj, r].astype(F32)
                    + self.fm[r].astype(F32) + self.fp[r].astype(F32))

    class Spread:
        def __init__(self, block, ssem, rsem, width):
            self.block, self.ssem, self.rsem = block, ssem, rsem
            self.A, self.B = pl.ds(0, width // 2), pl.ds(width // 2, width // 2)

        def c(self, i, c, j, dev, cols=None):
            ref = self.block(c, j)
            if cols is not None:
                ref = ref.at[..., cols]
            return remote(ref, ref, self.ssem.at[i], self.rsem.at[i], dev)

        def first(self):
            start(self.c(0, core, yj, dev_yp))
            start(self.c(1, core, yj, dev_ym))
            start(self.c(2, core, yj, dev_pair))

        def relay(self):
            self.c(0, core, ym, dev_yp).wait_recv()
            start(self.c(3, core, ym, dev_yp, self.A))
            start(self.c(4, core, ym, dev_pair))
            self.c(1, core, yp, dev_ym).wait_recv()
            start(self.c(5, core, yp, dev_ym, self.B))
            start(self.c(6, core, yp, dev_pair))

        def relay2(self):
            self.c(3, core, yo, dev_yp, self.A).wait_recv()
            start(self.c(7, core, yo, dev_pair, self.A))
            self.c(5, core, yo, dev_ym, self.B).wait_recv()
            start(self.c(8, core, yo, dev_pair, self.B))

        def finish(self):
            self.c(2, 1 - core, yj, dev_pair).wait_recv()
            self.c(4, 1 - core, ym, dev_pair).wait_recv()
            self.c(6, 1 - core, yp, dev_pair).wait_recv()
            self.c(7, 1 - core, yo, dev_pair, self.A).wait_recv()
            self.c(8, 1 - core, yo, dev_pair, self.B).wait_recv()

    blk1 = blk // 2

    def start1(u, c, j):
        return u * half_tok + c * (half_tok // 2) + j * blk1

    def rows1(u, c, j):
        return pl.ds(pl.multiple_of(start1(u, c, j), blk1), blk1)

    red1 = [Reduce(functools.partial(lambda u, c, j: part1.at[rows1(u, c, j)], u),
                   prx1.at[u], ps1.at[u], rA1.at[u], rB1.at[u], sA1.at[u], sB1.at[u],
                   fm1.at[u], fp1.at[u], rs1_s.at[u], rs1_r.at[u]) for u in range(2)]
    spr1 = [Spread(functools.partial(lambda u, c, j: n2.at[rows1(u, c, j)], u),
                   ag1_s.at[u], ag1_r.at[u], dim) for u in range(2)]

    def project1(u, c):
        n = half_tok // 2
        rows = pl.ds(pl.multiple_of(start1(u, c, 0), n), n)
        zb[rows, :] = keep(mm(att[rows, :], ao[...]), rows)

        @pl.loop(0, SIDE)
        def _(x):
            kdim = att.shape[1]
            cols = [wo[x, z].reshape(kdim, HD) for z in range(SIDE)]
            n = pl.ds(pl.multiple_of(x * SIDE * HD, SIDE * HD), SIDE * HD)
            acc = mm(att[rows, :], jnp.concatenate(cols, axis=1)) + mm(zb[rows, :], bo[:, n])
            part1[rows, n] = acc.astype(BF)

    own_rows = 16

    def residual1(u):
        red1[u].finish()

        @pl.loop(0, blk1 // own_rows)
        def _(i):
            r0 = pl.multiple_of(i * own_rows, own_rows)
            src = pl.ds(pl.multiple_of(start1(u, core, yj) + r0, own_rows), own_rows)
            h_new = tok[src, :].astype(F32) + red1[u].total(pl.ds(r0, own_rows))
            hs[u, pl.ds(r0, own_rows), :] = h_new
            n2[src, :] = norm_rows(h_new)

        spr1[u].first()

    for name in ("ao", "bo"):
        loads[name].wait()
    g_done("wo")
    project1(0, 1 - core)
    red1[0].send_pair()
    project1(0, core)
    project1(1, 1 - core)
    red1[1].send_pair()
    red1[0].ring1()
    project1(1, core)
    red1[1].ring1()
    red1[0].ring2()
    red1[1].ring2()
    g_f2("wg")
    d_s2()
    residual1(0)
    residual1(1)
    spr1[0].relay()
    spr1[1].relay()
    spr1[0].relay2()
    spr1[1].relay2()
    for name in ("ag", "bg", "au", "bu", "ad", "bd"):
        loads[name].wait()
    spr1[0].finish()
    spr1[1].finish()

    @pl.loop(0, 2)
    def _(i):
        rows = pl.ds(pl.multiple_of(i * half_tok, half_tok), half_tok)
        zg[rows, :] = keep(mm(n2[rows, :], ag[...]), rows)
        zu[rows, :] = keep(mm(n2[rows, :], au[...]), rows)

    g_done("wg")
    ff = wg.shape[-1]
    ft = 256

    @pl.loop(0, ff // ft)
    def _(f):
        cols = pl.ds(pl.multiple_of(f * ft, ft), ft)
        wgc = wg[:, :, :, cols].reshape(dim, ft)
        wuc = wu[:, :, :, cols].reshape(dim, ft)
        for t in range(2):
            rows = pl.ds(t * half_tok, half_tok)
            g = mm(n2[rows, :], wgc) + mm(zg[rows, :], bg[:, cols])
            u = mm(n2[rows, :], wuc) + mm(zu[rows, :], bu[:, cols])
            hid[:, t, :, cols] = (g / (1.0 + jnp.exp(-g)) * u).astype(BF).reshape(2, half_tok // 2, ft)

    for i in range(2):
        rows = pl.ds(i * half_tok, half_tok)
        low = keep(mm(hid[:, i].reshape(half_tok, ff), ad[...]), rows)
        zd[:, i] = low.reshape(2, half_tok // 2, low.shape[1])

    zs = [lax.rem(zi + k, SIDE) for k in (0, 1, 3, 2)]
    xs = [lax.rem(xi + k, SIDE) for k in (0, 1, 3, 2)]
    n_unit = 4

    def slots(u):
        return [(0, zs[u], k, (2 * k + lax.rem(zs[u], 2)) * SIDE + zs[u]) for k in range(2)] + [
            (1, xs[u], k, xs[u] * SIDE + 2 * k + lax.rem(xs[u] + 1, 2)) for k in range(2)]

    def lanes(slot):
        return pl.ds(pl.multiple_of(slot * HD, HD), HD)

    red2 = [Reduce(functools.partial(lambda u, c, j: part2.at[u, c, j], u),
                   prx2.at[u], ps2.at[u], rA2.at[u], rB2.at[u], sA2.at[u], sB2.at[u],
                   fm2.at[u], fp2.at[u], rs2_s.at[u], rs2_r.at[u]) for u in range(n_unit)]
    spr2 = [Spread(functools.partial(lambda u, c, j: outb.at[u, c, j], u),
                   ag2_s.at[u], ag2_r.at[u], dim // n_unit) for u in range(n_unit)]

    def project2(u):
        wcol = jnp.concatenate([wd[s, g, k] for s, g, k, _ in slots(u)], axis=1)
        bcol = jnp.concatenate([bd[:, lanes(n)] for _, _, _, n in slots(u)], axis=1)
        for own in range(2):
            c = core if own else 1 - core
            acc = mm(hid[c].reshape(half_tok, ff), wcol) + mm(zd[c].reshape(half_tok, zd.shape[3]), bcol)
            acc = acc.astype(BF)
            for t in range(2):
                for j in range(RING_Y):
                    r0 = (t * RING_Y + j) * blk1
                    part2[u, c, j, t] = acc[r0:r0 + blk1]
            if not own:
                red2[u].send_pair()

    def residual2(u):
        red2[u].finish()
        old = jnp.concatenate([hs[:, :, lanes(n)] for _, _, _, n in slots(u)], axis=2)
        outb[u, core, yj] = (old + red2[u].total(slice(None))).astype(BF)
        spr2[u].first()

    outs = []

    def store2(u):
        spr2[u].finish()
        for q, (_, _, _, n) in enumerate(slots(u)):
            for t in range(2):
                o = pltpu.make_async_copy(outb.at[u, :, :, t, :, pl.ds(q * HD, HD)],
                                          out_h.at[t, :, :, :, lanes(n)], osem.at[u, q, t])
                o.start()
                outs.append(o)

    project2(0)
    red2[0].ring1()
    red2[0].ring2()
    g_f2("wd")
    d_got(4)
    project2(1)
    residual2(0)
    red2[1].ring1()
    project2(2)
    spr2[0].relay()
    red2[1].ring2()
    red2[2].ring1()
    spr2[0].relay2()
    d_got(5)
    project2(3)
    residual2(1)
    red2[2].ring2()
    red2[3].ring1()
    spr2[1].relay()
    store2(0)
    residual2(2)
    red2[3].ring2()
    spr2[1].relay2()
    spr2[2].relay()
    residual2(3)
    store2(1)
    spr2[2].relay2()
    spr2[3].relay()
    store2(2)
    spr2[3].relay2()
    store2(3)
    for o in outs:
        o.wait()
    for c in sent:
        c.wait_send()


def body(
    tokens, lengths, request_adapter, w_qkv, w_out, w_gate, w_up, w_down,
    a_qkv, b_qkv, a_out, b_out, a_gate, b_gate, a_up, b_up, a_down, b_down,
):
    n_tok, dim = tokens.shape
    kq, _, lw = w_qkv.shape
    ff = w_gate.shape[1]
    nz = a_qkv.shape[1]
    b1 = n_tok // 16
    V = pltpu.VMEM
    scratch = [
        V((SIDE, SIDE, 3, kq, lw), BF),
        V((SIDE, SIDE, 2, w_out.shape[0] // 2, w_out.shape[1]), BF),
        V((SIDE, SIDE, w_gate.shape[0], ff), BF),
        V((SIDE, SIDE, w_up.shape[0], ff), BF),
        V((2, SIDE, 2) + w_down.shape, BF),
        V(a_qkv.shape, BF), V((3, nz, lw), BF), V(a_out.shape, BF), V(b_out.shape, BF),
        V(a_gate.shape, BF), V(b_gate.shape, BF), V(a_up.shape, BF), V(b_up.shape, BF),
        V(a_down.shape, BF), V(b_down.shape, BF),
        V((n_tok, dim), BF), V((n_tok, dim), BF), V((n_tok, dim), BF),
        V((4, 2, 4, 2, b1, dim // 4), BF), V((n_tok, dim), BF), V((4, 2, 4, 2, b1, dim // 4), BF),
        V((2, 4, b1, dim), BF), V((4, 4, 2, b1, dim // 4), BF),
        V((2, 4, b1, dim), BF), V((4, 4, 2, b1, dim // 4), BF),
    ]
    scratch += [V((2, b1, dim // 2), BF)] * 2 + [V((4, 2, b1, dim // 8), BF)] * 2
    scratch += [V((2, b1, dim // 2), BF)] * 2 + [V((4, 2, b1, dim // 8), BF)] * 2
    scratch += [V((2, b1, dim), BF)] * 2 + [V((4, 2, b1, dim // 4), BF)] * 2
    scratch += [
        V((n_tok, nz), BF), V((n_tok, nz), BF), V((n_tok, nz), BF), V((n_tok, nz), BF), V((2, 2, n_tok // 4, nz), BF),
        V((3, lw // HD, n_tok, HD), BF), V((n_tok, lw), BF), V((2, 2, n_tok // 4, ff), BF), V((2, b1, dim), F32),
        V((n_tok, HD), F32), V((n_tok, HD), F32), V((n_tok, HD), jnp.int32), V((n_tok, HD), jnp.int32),
    ]
    D = pltpu.SemaphoreType.DMA
    scratch += [D((4, 2, 6)), D((4, 2, 6)), D((2, 10)), D((2, 10)), D((2, 9)), D((2, 9)),
                D((4, 10)), D((4, 10)), D((4, 9)), D((4, 9)), D((24,)), D((4, 4, 2))]
    smem = pl.BlockSpec(memory_space=pltpu.SMEM)
    hbm = pl.BlockSpec(memory_space=pl.ANY)
    out = pl.pallas_call(
        kernel,
        out_shape=jax.ShapeDtypeStruct((2, 2, 4, b1, dim), BF),
        in_specs=[smem, smem] + [hbm] * 16,
        out_specs=hbm,
        scratch_shapes=scratch,
        compiler_params=pltpu.CompilerParams(
            collective_id=0, has_side_effects=True, vmem_limit_bytes=67043328),
        name="layer",
    )(
        lengths, request_adapter, tokens,
        w_qkv.transpose(1, 0, 2),
        w_out.reshape(2, w_out.shape[0] // 2, w_out.shape[1]),
        w_gate, w_up, w_down,
        a_qkv, b_qkv.transpose(1, 0, 2), a_out, b_out, a_gate, b_gate, a_up, b_up, a_down, b_down,
    )
    return out.reshape(n_tok, dim)


def solution(mesh):
    in_specs = (
        P("req", None), P("req", None), P("req", None), P("req", None, "tp"), P("tp", "req"),
        P("req", "tp"), P("req", "tp"), P("tp", "req"), P(), P(None, None, "tp"), P("tp", None),
        P(), P(), P(None, "tp"), P(), P(None, "tp"), P("tp", None), P(),
    )
    return jax.shard_map(body, mesh=mesh, in_specs=in_specs, out_specs=P("req", None), check_vma=False)
```
